32 devices in a mesh: slab: 8 (over z, x), head: 4 (over y, core).
Axes of the slice: x: 2, y: 2, z: 4, core: 2. Of those that a mesh axis runs over, the one named last changes fastest.
Arguments:
- atom_feats: bfloat16 [2, 4096, 128], P(None, 'slab'), may hold values from -16 to 16
- pair_feats: bfloat16 [4096, 16, 128], P('slab'), may hold values from -8 to 330
- tok_slot: int32 [4096], P('slab'), may hold values from 0 to 255, as said below
- w_proj: bfloat16 [4, 128, 128], P(None, None, 'head'), may hold values from -0.5 to 0.5
- w_out: bfloat16 [128, 128], P('head'), may hold values from -0.5 to 0.5
- w_pair: bfloat16 [16, 4], P(None, 'head'), may hold values from -1.2 to 1.2
- w_tok: bfloat16 [128, 768], P(None, 'head'), may hold values from -0.5 to 0.5
- d_tok: bfloat16 [2, 256, 768], P(None, 'slab', 'head'), may hold values from -6 to 6
Outputs:
- tok_act: bfloat16 [2, 256, 768], P(None, 'slab', 'head')
- grad_proj: float32 [4, 128, 128], P(None, None, 'head')
- grad_out: float32 [128, 128], P('head')
- grad_pair: float32 [16, 4], P(None, 'head')
- grad_tok: float32 [128, 768], P(None, 'head')
The draws below stay inside these ranges and needn't reach their ends.
Inputs may be any that keep to these rules, and one draw needn't show every extreme that they name: `tok_slot`: never falling. The atoms s * 512 to (s + 1) * 512 - 1 use slots s * 32 to s * 32 + n - 1, each at least once, with n from 16 to 32; the first of these atoms is in slot s * 32. The last slab and one other use all 32 slots.
All inputs are finite; a program needn't handle non-finite values.
Results may differ from the reference program's by a relative error of at most 0.023.
Values may be sent and summed in bfloat16 or wider, within the bound.
A program may use at most 64 MiB of HBM per device.

```python
import math
import jax
import jax.numpy as jnp
from jax import lax

ATOM_W = 128
TOKEN_W = 768
HEADS = 4
HEAD_FEATURES = 32
PAIR_C = 16
Q_WIN = 32
K_WIN = 128
RIM = 48
SAMPLES = 2
ATOM_DEV = 512
TOK_CAP = 32
ATOM_TOTAL = 4096
TOKENS = 256


def draw_atom_feats(key, part):
    key_list = jax.random.split(key, 3)
    spread = math.log(10.0)
    row_scale = jnp.exp(jax.random.uniform(key_list[1], (1, ATOM_TOTAL, 1)) * spread) / 10.0 ** 0.5
    column_scale = jnp.exp(jax.random.uniform(key_list[2], (1, 1, ATOM_W)) * spread) / 10.0 ** 0.5
    values = jax.random.normal(key_list[0], (SAMPLES, ATOM_TOTAL, ATOM_W)) * row_scale * column_scale
    return jnp.clip(values, -16.0, 16.0).astype(jnp.bfloat16)


def draw_pair_feats(key, part):
    key_list = jax.random.split(key, 1)
    values = jax.random.normal(key_list[0], (ATOM_TOTAL, PAIR_C, K_WIN))
    return jnp.clip(values, -8.0, 330.0).astype(jnp.bfloat16)


def draw_w_pair(key, part):
    key_list = jax.random.split(key, 2)
    values = jax.random.normal(key_list[0], (PAIR_C, HEADS)) * PAIR_C ** (-0.5)
    leading = jax.random.uniform(key_list[1], (1, HEADS), minval=0.8, maxval=1.2)
    channel = jnp.arange(PAIR_C, dtype=jnp.int32)[:, None]
    values = jnp.where(channel == 0, leading, values)
    return jnp.clip(values, -1.2, 1.2).astype(jnp.bfloat16)


def draw_tok_slot(key, part):
    slab_total = ATOM_TOTAL // ATOM_DEV
    key_list = jax.random.split(key, 3)
    used = jax.random.randint(key_list[0], (slab_total,), TOK_CAP // 2, TOK_CAP + 1)
    full_slab = jax.random.randint(key_list[1], (), 0, slab_total)
    slab_ids = jnp.arange(slab_total, dtype=jnp.int32)
    used = jnp.where((slab_ids == full_slab) | (slab_ids == slab_total - 1), TOK_CAP, used)
    order = jax.vmap(lambda sub_key: jax.random.permutation(sub_key, ATOM_DEV))(jax.random.split(key_list[2], slab_total))
    order = order.astype(jnp.int32)
    first_value = order[:, :1]
    order = jnp.where(order == 0, first_value, order)
    order = order.at[:, 0].set(0)
    starts = (order < used[:, None]).astype(jnp.int32)
    ranking = jnp.cumsum(starts, axis=1)
    slots = slab_ids[:, None] * TOK_CAP + ranking - 1
    return slots.reshape(-1).astype(jnp.int32)


def levels(stream_key, extent, cuts, smallest, high):
    loudness, own = 1.0, jax.random.fold_in(stream_key, 6)
    for axis_at, shards_of in cuts:
        draws = jnp.exp(jax.random.uniform(jax.random.fold_in(own, axis_at), (shards_of,), jnp.float32, smallest / len(cuts), high / len(cuts)))
        loudness = loudness * jnp.repeat(draws, extent[axis_at] // shards_of).reshape([-1 if axis == axis_at else 1 for axis in range(len(extent))])
    return loudness


def gaussian(rng, extent, width, reach, shards=(), kind=jnp.bfloat16):
    entries = width * jax.random.normal(rng, extent, jnp.float32)
    if shards:
        entries = entries * levels(rng, extent, shards, -0.22, 0.18)
    return jnp.clip(entries, -reach, reach).astype(kind)


def setup_inputs(seed: int = 0) -> dict:
    seeds = jax.random.split(jax.random.key(seed), 9)
    atom_feats = draw_atom_feats(jax.random.fold_in(seeds[8], 71), 0)
    pair_feats = draw_pair_feats(jax.random.fold_in(seeds[8], 71), 0)
    tok_slot = draw_tok_slot(jax.random.fold_in(seeds[8], 71), 0)
    w_proj = gaussian(seeds[3], (4, ATOM_W, HEADS * HEAD_FEATURES), ATOM_W ** -0.5, 0.5, ((2, 4),))
    w_out = gaussian(seeds[4], (HEADS * HEAD_FEATURES, ATOM_W), (HEADS * HEAD_FEATURES) ** -0.5, 0.5, ((0, 4),))
    w_pair = draw_w_pair(jax.random.fold_in(seeds[8], 71), 0)
    w_tok = gaussian(seeds[6], (ATOM_W, TOKEN_W), ATOM_W ** -0.5, 0.5, ((1, 4),))
    d_tok = gaussian(seeds[7], (SAMPLES, TOKENS, TOKEN_W), 1.0, 6.0, ((1, 8), (2, 4)))
    return {"atom_feats": atom_feats, "pair_feats": pair_feats, "tok_slot": tok_slot, "w_proj": w_proj, "w_out": w_out, "w_pair": w_pair, "w_tok": w_tok, "d_tok": d_tok}


EPSILON = 1e-05

def key_windows(extended, block_count):
    row_total = block_count * Q_WIN
    pieces = []
    for offset in range(K_WIN // Q_WIN):
        segment = extended[Q_WIN * offset:Q_WIN * offset + row_total]
        pieces.append(segment.reshape((block_count, Q_WIN) + extended.shape[1:]))
    return jnp.concatenate(pieces, axis=1)

def key_unwindowed_rows(windowed, block_count):
    row_total = block_count * Q_WIN
    margin = K_WIN - Q_WIN
    summed = None
    for offset in range(K_WIN // Q_WIN):
        segment = windowed[:, Q_WIN * offset:Q_WIN * (offset + 1)].reshape((row_total,) + windowed.shape[2:])
        segment = jnp.pad(segment, ((Q_WIN * offset, margin - Q_WIN * offset), (0, 0)))
        summed = segment if summed is None else summed + segment
    return summed[RIM:RIM + row_total]

def reference(atom_feats, pair_feats, tok_slot, w_proj, w_out, w_pair, w_tok, d_tok):
    block_count = ATOM_TOTAL // Q_WIN
    score_scale = HEAD_FEATURES ** (-0.5)
    factor = (SAMPLES * ATOM_TOTAL) ** (-0.5)
    group_width = TOKEN_W // HEADS
    positions = Q_WIN * jnp.arange(block_count, dtype=jnp.int32)[:, None] - RIM + jnp.arange(K_WIN, dtype=jnp.int32)[None, :]
    in_range = (positions >= 0) & (positions < ATOM_TOTAL)
    pair_bias_terms = jnp.einsum('icj,ch->hij', pair_feats.astype(jnp.float32), w_pair.astype(jnp.float32))
    pair_bias_terms = pair_bias_terms.reshape(HEADS, block_count, Q_WIN, K_WIN)
    counts = jax.ops.segment_sum(jnp.ones((ATOM_TOTAL,), jnp.float32), tok_slot, TOKENS)
    divisor = jnp.maximum(counts, 1.0)

    def one_sample(running, inputs):
        grad_proj, grad_out, grad_tok, bias_sum = running
        sample_feats, sample_cot = inputs
        feats_float = sample_feats.astype(jnp.float32)
        centered = feats_float - lax.optimization_barrier(jnp.mean(feats_float, axis=1, keepdims=True))
        variance = lax.optimization_barrier(jnp.mean(centered * centered, axis=1, keepdims=True))
        normed = (centered * lax.rsqrt(variance + EPSILON)).astype(jnp.bfloat16)
        projected = [jnp.dot(normed, w_proj[which], preferred_element_type=jnp.float32) for which in range(4)]
        queries = (projected[0] * score_scale).astype(jnp.bfloat16)
        keys_all = projected[1].astype(jnp.bfloat16)
        values_all = projected[2].astype(jnp.bfloat16)
        gating = jax.nn.sigmoid(projected[3])
        attn_sum = jnp.zeros((ATOM_TOTAL, ATOM_W), jnp.float32)
        kept_state = []
        for head_position in range(HEADS):
            columns = slice(head_position * HEAD_FEATURES, (head_position + 1) * HEAD_FEATURES)
            query_block_rows = queries[:, columns].astype(jnp.float32).reshape(block_count, Q_WIN, HEAD_FEATURES)
            key_window_rows = key_windows(jnp.pad(keys_all[:, columns], ((RIM, RIM), (0, 0))), block_count).astype(jnp.float32)
            value_window_rows = key_windows(jnp.pad(values_all[:, columns], ((RIM, RIM), (0, 0))), block_count).astype(jnp.float32)
            attention_scores = jnp.einsum('yeh,yjh->yej', query_block_rows, key_window_rows) + pair_bias_terms[head_position]
            attention_scores = jnp.where(in_range[:, None, :], attention_scores, -jnp.inf)
            highest = lax.optimization_barrier(jnp.max(attention_scores, axis=2, keepdims=True))
            exponent = jnp.exp(attention_scores - highest)
            attn_weights = exponent / lax.optimization_barrier(jnp.sum(exponent, axis=2, keepdims=True))
            weight_half_precision = attn_weights.astype(jnp.bfloat16)
            attended_output = jnp.einsum('mxh,mhr->mxr', weight_half_precision.astype(jnp.float32), value_window_rows).reshape(ATOM_TOTAL, HEAD_FEATURES)
            heads_out = (gating[:, columns] * attended_output).astype(jnp.bfloat16)
            head_part = jnp.dot(heads_out, w_out[columns], preferred_element_type=jnp.float32)
            attn_sum = attn_sum + lax.optimization_barrier(head_part.astype(jnp.bfloat16)).astype(jnp.float32)
            kept_state.append((query_block_rows, key_window_rows, value_window_rows, attn_weights, weight_half_precision, attended_output, heads_out))
        mixed_half = (feats_float + attn_sum).astype(jnp.bfloat16)
        pre_act = jnp.dot(mixed_half, w_tok, preferred_element_type=jnp.float32)
        act_gate = jax.nn.sigmoid(pre_act)
        atom_act = (pre_act * act_gate).astype(jnp.bfloat16)
        token_sums = jax.ops.segment_sum(atom_act.astype(jnp.float32), tok_slot, TOKENS)
        tok_act = (token_sums / divisor[:, None]).astype(jnp.bfloat16)
        tok_grad = (sample_cot.astype(jnp.float32) / divisor[:, None]).astype(jnp.bfloat16)
        slope = act_gate * (1.0 + pre_act * (1.0 - act_gate))
        act_grad = (tok_grad[tok_slot].astype(jnp.float32) * slope).astype(jnp.bfloat16)
        grad_tok = grad_tok + jnp.dot(mixed_half.T, act_grad, preferred_element_type=jnp.float32)
        mixed_total = jnp.zeros((ATOM_TOTAL, ATOM_W), jnp.float32)
        for head_position in range(HEADS):
            columns = slice(head_position * group_width, (head_position + 1) * group_width)
            head_part = jnp.dot(act_grad[:, columns], w_tok[:, columns].T, preferred_element_type=jnp.float32)
            mixed_total = mixed_total + lax.optimization_barrier(head_part.astype(jnp.bfloat16)).astype(jnp.float32)
        mixed_grad = mixed_total.astype(jnp.bfloat16)
        for head_position in range(HEADS):
            columns = slice(head_position * HEAD_FEATURES, (head_position + 1) * HEAD_FEATURES)
            query_block_rows, key_window_rows, value_window_rows, attn_weights, weight_half_precision, attended_output, heads_out = kept_state[head_position]
            head_gate = gating[:, columns]
            out_grad = jnp.dot(mixed_grad, w_out[columns].T, preferred_element_type=jnp.float32)
            grad_out = grad_out.at[columns].add(jnp.dot(heads_out.T, mixed_grad, preferred_element_type=jnp.float32))
            att_grad = (head_gate * out_grad).astype(jnp.bfloat16)
            gate_grad = (out_grad * attended_output * head_gate * (1.0 - head_gate)).astype(jnp.bfloat16)
            attention_block_rows = att_grad.astype(jnp.float32).reshape(block_count, Q_WIN, HEAD_FEATURES)
            probability_gradient = jnp.einsum('yeh,yjh->yej', attention_block_rows, value_window_rows)
            score_grad = attn_weights * (probability_gradient - lax.optimization_barrier(jnp.sum(attn_weights * probability_gradient, axis=2, keepdims=True)))
            score_single_precision = score_grad.astype(jnp.bfloat16).astype(jnp.float32)
            query_gradient = (score_scale * jnp.einsum('mxh,mhr->mxr', score_single_precision, key_window_rows)).reshape(ATOM_TOTAL, HEAD_FEATURES).astype(jnp.bfloat16)
            key_gradient = key_unwindowed_rows(jnp.einsum('gys,gyp->gsp', score_single_precision, query_block_rows), block_count).astype(jnp.bfloat16)
            value_gradient = key_unwindowed_rows(jnp.einsum('gys,gyp->gsp', weight_half_precision.astype(jnp.float32), attention_block_rows), block_count).astype(jnp.bfloat16)
            for which, grad_part in enumerate((query_gradient, key_gradient, value_gradient, gate_grad)):
                grad_proj = grad_proj.at[which, :, columns].add(jnp.dot(normed.T, grad_part, preferred_element_type=jnp.float32))
            bias_sum = bias_sum.at[head_position].add(score_single_precision.reshape(ATOM_TOTAL, K_WIN))
        return ((grad_proj, grad_out, grad_tok, bias_sum), tok_act)
    initial = (jnp.zeros((4, ATOM_W, HEADS * HEAD_FEATURES), jnp.float32), jnp.zeros((HEADS * HEAD_FEATURES, ATOM_W), jnp.float32), jnp.zeros((ATOM_W, TOKEN_W), jnp.float32), jnp.zeros((HEADS, ATOM_TOTAL, K_WIN), jnp.float32))
    totals, tok_act = lax.scan(one_sample, initial, (atom_feats, d_tok))
    grad_proj, grad_out, grad_tok, bias_sum = totals
    bias_grad = lax.optimization_barrier(bias_sum.astype(jnp.bfloat16)).astype(jnp.float32)
    grad_pair = jnp.einsum('icj,hij->ch', pair_feats.astype(jnp.float32), bias_grad)
    return (tok_act, grad_proj * factor, grad_out * factor, grad_pair * factor, grad_tok * factor)
```

```python
import functools
import jax
import jax.numpy as jnp
from jax import lax
from jax.experimental import pallas as pl
from jax.experimental.pallas import tpu as pltpu
from jax.sharding import PartitionSpec as P

Q_WIN = 32
K_WIN = 128
RIM = 48
EPSILON = 1e-05
MASKED = -1e30
BF = jnp.bfloat16
F32 = jnp.float32
NT = (((1,), (1,)), ((), ()))
NN = (((1,), (0,)), ((), ()))
TN = (((0,), (0,)), ((), ()))


def mm(a, b, dims=NN):
    return lax.dot_general(a, b, dims, preferred_element_type=F32)


def iota(shape, dim):
    return lax.broadcasted_iota(jnp.int32, shape, dim)


def layer_norm(x):
    x = x.astype(F32)
    centered = x - jnp.mean(x, axis=-1, keepdims=True)
    variance = jnp.mean(centered * centered, axis=-1, keepdims=True)
    return (centered * lax.rsqrt(variance + EPSILON)).astype(BF)


def kernel(
    n, heads, inner,
    feats, pair_any, slot, wproj, wout, wpair, wtok, dtok,
    tok_out, gproj_out, gout_out, gpair_out, gtok_out,
    pair, halo, nx, wo, wbig, bdqg, bdk, bdv, bias, ncat, gate, qp, ucat, prob, zcat, att,
    hbuf, mhs, acts, ags, mtc, og0, osend, orecv, agp, ggp, qgp, ycat,
    gosend, gorecv, ebuf, erecv, eres, lbuf, lrecv, precv, lres, xbuf,
    pair_sem, halo_sem, wo_sem, h_sem, o_sem, go_sem, e_sem, eg_sem, l_sem, lp_sem, lg_sem, x_sem,
):
    samples, atoms, width = feats.shape
    depth = wproj.shape[2]
    lanes = width
    groups = lanes // depth
    step = groups * Q_WIN
    chunks = atoms // step
    rows = samples * Q_WIN
    slots = dtok.shape[1]
    channels = wpair.shape[0]
    token_cols = wtok.shape[1]
    scale = depth ** (-0.5)
    factor = (samples * atoms * n) ** (-0.5)
    outer = n // inner
    me_s = lax.axis_index("slab")
    me_h = lax.axis_index("head")
    own = lax.rem(me_s, inner)
    base = me_s - own
    sends = []

    def head_peer(k):
        return {"head": lax.rem(me_h + k + heads, heads)}

    def inner_peer(k):
        return {"slab": base + lax.rem(own + k, inner)}

    def outer_peer(k):
        return {"slab": lax.rem(me_s + k * inner, n)}

    def ring_peer(k):
        return {"slab": lax.rem(me_s + k + n, n)}

    def send(src, dst, sems, index, device):
        copy = pltpu.make_async_remote_copy(
            src_ref=src, dst_ref=dst, send_sem=sems.at[(0,) + index], recv_sem=sems.at[(1,) + index],
            device_id=device, device_id_type=pl.DeviceIdType.MESH,
        )
        copy.start()
        sends.append(copy)
        return copy

    pair_copy = pltpu.make_async_copy(pair_any, pair, pair_sem)
    pair_copy.start()
    greeted = [head_peer(k) for k in range(1, heads)] + [inner_peer(k) for k in range(1, inner)]
    greeted += [outer_peer(k) for k in range(1, outer)]
    if outer > 1:
        greeted += [ring_peer(1), ring_peer(-1)]
    barrier = pltpu.get_barrier_semaphore()
    for device in greeted:
        pl.semaphore_signal(barrier, inc=1, device_id=device, device_id_type=pl.DeviceIdType.MESH)

    for s in range(samples):
        nx[s, RIM : RIM + atoms, :] = layer_norm(feats[s])
    lane_group = iota((lanes, lanes), 1) // depth
    row_group = iota((lanes, lanes), 0) // depth
    spreader = (lax.rem(iota((depth, lanes), 1), depth) == iota((depth, lanes), 0)).astype(F32).astype(BF)
    wide = [mm(wproj[f], spreader) for f in range(4)]
    for g in range(groups):
        keep = lane_group == g
        span = slice(g * lanes, (g + 1) * lanes)
        bdqg[span, :lanes] = jnp.where(keep, wide[0], 0.0).astype(BF)
        bdqg[span, lanes:] = jnp.where(keep, wide[3], 0.0).astype(BF)
        bdk[span, :] = jnp.where(keep, wide[1], 0.0).astype(BF)
        bdv[span, :] = jnp.where(keep, wide[2], 0.0).astype(BF)
    wo[0] = wout[...]

    pl.semaphore_wait(barrier, len(greeted))

    to_left = send(feats.at[:, 0:RIM, :], halo.at[1], halo_sem, (1,), ring_peer(-1))
    to_right = send(feats.at[:, atoms - RIM : atoms, :], halo.at[0], halo_sem, (0,), ring_peer(1))
    wo_copies = [send(wout, wo.at[k], wo_sem, (k - 1,), head_peer(k)) for k in range(1, heads)]

    for c in range(chunks):
        for s in range(samples):
            for g in range(groups):
                at = RIM + c * step + g * Q_WIN
                ncat[c * rows + s * Q_WIN : c * rows + (s + 1) * Q_WIN, g * lanes : (g + 1) * lanes] = nx[
                    s, at : at + Q_WIN, :
                ]
    projected = mm(ncat[...], bdqg[...])
    queries = (projected[:, :lanes] * scale).astype(BF)
    qp[...] = queries
    gate[...] = jax.nn.sigmoid(projected[:, lanes:])
    ucat[...] = mm(queries, bdk[...], NT).astype(BF)

    slot_ids = me_s * slots + iota((slots, atoms), 0)
    member = jnp.where(slot[...] == slot_ids, 1.0, 0.0)
    divisor = jnp.maximum(jnp.sum(member, axis=1, keepdims=True), 1.0)
    member = member.astype(BF)
    tok_grad = [(dtok[s].astype(F32) / divisor).astype(BF) for s in range(samples)]

    flat = Q_WIN * channels
    picker = lax.rem(iota((channels, flat), 1), channels) == iota((channels, flat), 0)
    w_wide = jnp.broadcast_to(wpair[...].astype(F32), (channels, Q_WIN)).astype(BF)
    w_rows = mm(w_wide, picker.astype(F32).astype(BF), TN)
    diagonal = iota((Q_WIN, flat), 1) // channels == iota((Q_WIN, flat), 0)
    mixer = jnp.where(diagonal, w_rows, 0.0).astype(BF)
    pair_copy.wait()
    for b in range(chunks * groups):
        bias[b] = mm(mixer, pair[b * flat : (b + 1) * flat, :])

    for k in range(heads):
        if k:
            wo_copies[k - 1].wait_recv()
        tall = jnp.concatenate([wo[k]] * groups, axis=0).astype(F32)
        for g in range(groups):
            wbig[k * lanes : (k + 1) * lanes, g * lanes : (g + 1) * lanes] = jnp.where(
                row_group == g, tall, 0.0
            ).astype(BF)

    to_right.wait_recv()
    to_left.wait_recv()
    for s in range(samples):
        nx[s, 0:RIM, :] = layer_norm(halo[0, s])
        nx[s, RIM + atoms : RIM + atoms + RIM, :] = layer_norm(halo[1, s])

    h_copies, o_copies = {}, {}

    def forward(c):
        at_rows = slice(c * rows, (c + 1) * rows)
        for s in range(samples):
            for g in range(groups):
                b = c * groups + g
                cols = slice(g * lanes, (g + 1) * lanes)
                here = slice(c * rows + s * Q_WIN, c * rows + (s + 1) * Q_WIN)
                window = nx[s, b * Q_WIN : b * Q_WIN + K_WIN, :]
                scores = mm(ucat[here, cols], window, NT) + bias[b]
                first = b * Q_WIN - RIM
                if first < 0 or first + K_WIN > atoms:
                    where = me_s * atoms + first + iota((Q_WIN, K_WIN), 1)
                    scores = jnp.where((where >= 0) & (where < atoms * n), scores, MASKED)
                top = jnp.max(scores, axis=1, keepdims=True)
                e = jnp.exp(scores - top)
                p = e / jnp.sum(e, axis=1, keepdims=True)
                prob[s, b] = p
                zcat[here, cols] = mm(p.astype(BF), window).astype(BF)
        attended = mm(zcat[at_rows, :], bdv[...])
        att[at_rows, :] = attended
        hbuf[0, c] = (gate[at_rows, :] * attended).astype(BF)
        h_copies[c] = [
            send(hbuf.at[0, c], hbuf.at[k, c], h_sem, (k - 1, c), head_peer(k)) for k in range(1, heads)
        ]

    def middle(c):
        for copy in h_copies[c]:
            copy.wait_recv()
        mixed = mm(jnp.concatenate([hbuf[k, c] for k in range(heads)], axis=1), wbig[...])
        for s in range(samples):
            parts = [mixed[s * Q_WIN : (s + 1) * Q_WIN, g * lanes : (g + 1) * lanes] for g in range(groups)]
            span = slice(c * step, (c + 1) * step)
            half = (feats[s, span, :].astype(F32) + jnp.concatenate(parts, axis=0)).astype(BF)
            mhs[s, span, :] = half
            pre = mm(half, wtok[...])
            g1 = jax.nn.sigmoid(pre)
            acts[s, span, :] = (pre * g1).astype(BF)
            spread = mm(member[:, span], tok_grad[s], TN)
            ag = (spread * (g1 * (1.0 + pre * (1.0 - g1)))).astype(BF)
            ags[s, span, :] = ag
            mt = mm(ag, wtok[...], NT).astype(BF)
            for g in range(groups):
                mtc[c * rows + s * Q_WIN : c * rows + (s + 1) * Q_WIN, g * lanes : (g + 1) * lanes] = mt[
                    g * Q_WIN : (g + 1) * Q_WIN, :
                ]
        og = mm(mtc[c * rows : (c + 1) * rows, :], wbig[...], NT)
        og0[c] = og[:, :lanes]
        o_copies[c] = []
        for k in range(1, heads):
            osend[k - 1, c] = og[:, k * lanes : (k + 1) * lanes].astype(BF)
            o_copies[c].append(send(osend.at[k - 1, c], orecv.at[k - 1, c], o_sem, (k - 1, c), head_peer(-k)))

    def diagonal_sum(a):
        total = a[0:depth, 0:lanes]
        for g in range(1, groups):
            total = total + a[g * depth : (g + 1) * depth, g * lanes : (g + 1) * lanes]
        return total

    pair_terms = [None]

    def backward(c):
        at_rows = slice(c * rows, (c + 1) * rows)
        for copy in o_copies[c]:
            copy.wait_recv()
        og = og0[c]
        for k in range(1, heads):
            og = og + orecv[k - 1, c].astype(F32)
        gt = gate[at_rows, :]
        ag = (gt * og).astype(BF)
        agp[at_rows, :] = ag
        ggp[at_rows, :] = (og * att[at_rows, :] * gt * (1.0 - gt)).astype(BF)
        tcat = mm(ag, bdv[...], NT).astype(BF)
        for g in range(groups):
            b = c * groups + g
            cols = slice(g * lanes, (g + 1) * lanes)
            both = None
            for s in range(samples):
                here = slice(c * rows + s * Q_WIN, c * rows + (s + 1) * Q_WIN)
                window = nx[s, b * Q_WIN : b * Q_WIN + K_WIN, :]
                dp = mm(tcat[s * Q_WIN : (s + 1) * Q_WIN, cols], window, NT)
                p = prob[s, b]
                ds = (p * (dp - jnp.sum(p * dp, axis=1, keepdims=True))).astype(BF)
                ycat[here, cols] = mm(ds, window).astype(BF)
                ds = ds.astype(F32)
                both = ds if both is None else both + ds
            term = mm(both.astype(BF), pair[b * flat : (b + 1) * flat, :], NT)
            pair_terms[0] = term if pair_terms[0] is None else pair_terms[0] + term
        qgp[at_rows, :] = (scale * mm(ycat[at_rows, :], bdk[...])).astype(BF)

    order = []
    for t in range(chunks + 3):
        if t < chunks:
            order.append((forward, t))
        if 0 <= t - 1 < chunks:
            order.append((middle, t - 1))
        if t - 3 >= 0:
            order.append((backward, t - 3))
    late = [entry for entry in order if entry[0] is backward][1:]
    for step_of, c in [entry for entry in order if entry not in late]:
        step_of(c)

    hcat = jnp.concatenate(
        [jnp.concatenate([hbuf[k, c] for c in range(chunks)], axis=0) for k in range(heads)], axis=1
    )
    go_copies = []
    cross = mm(hcat, mtc[...], TN)
    go_own = diagonal_sum(cross[0:lanes])
    for k in range(1, heads):
        gosend[k - 1] = diagonal_sum(cross[k * lanes : (k + 1) * lanes]).astype(BF)
        go_copies.append(send(gosend.at[k - 1], gorecv.at[k - 1], go_sem, (k - 1,), head_peer(-k)))

    gtok = None
    for s in range(samples):
        sums = mm(member, acts[s])
        tok_out[s] = (sums / divisor).astype(BF)
        term = mm(ags[s], mhs[s], TN)
        gtok = term if gtok is None else gtok + term

    half_late = len(late) // 2
    for step_of, c in late[:half_late]:
        step_of(c)

    def exchange_outer(value, where):
        if outer == 1:
            return value
        xbuf[where, 0, : value.shape[0], :] = value.astype(BF)
        copies = [
            send(xbuf.at[where, 0], xbuf.at[where, k], x_sem, (where, k - 1), outer_peer(k)) for k in range(1, outer)
        ]
        for k in range(1, outer):
            copies[k - 1].wait_recv()
            value = value + xbuf[where, k, : value.shape[0], :].astype(F32)
        return value

    def scatter(buf, recv, sems):
        return [
            send(buf.at[lax.rem(own + k, inner)], recv.at[k - 1], sems, (k - 1,), inner_peer(k))
            for k in range(1, inner)
        ]

    def total_of(copies, value, recv):
        for k in range(1, inner):
            copies[k - 1].wait_recv()
            value = value + recv[k - 1].astype(F32)
        return value

    def gather(res, value, sems):
        res[own] = value.astype(BF)
        return [send(res.at[own], res.at[own], sems, (k - 1,), inner_peer(k)) for k in range(1, inner)]

    for k in range(1, heads):
        go_copies[k - 1].wait_recv()
        go_own = go_own + gorecv[k - 1].astype(F32)
    piece = ebuf.shape[1]
    parts = [gtok, go_own]
    spare = inner * piece - token_cols - depth
    if spare:
        parts.append(jnp.zeros((spare, lanes), F32))
    e_rows = jnp.concatenate(parts, axis=0).astype(BF)
    for j in range(inner):
        ebuf[j] = e_rows[j * piece : (j + 1) * piece]
    e_copies = scatter(ebuf, erecv, e_sem)

    for step_of, c in late[half_late:]:
        step_of(c)

    l_rows = jnp.concatenate(
        [
            diagonal_sum(mm(qgp[...], ncat[...], TN)),
            diagonal_sum(mm(qp[...], ycat[...], TN)),
            diagonal_sum(mm(agp[...], zcat[...], TN)),
            diagonal_sum(mm(ggp[...], ncat[...], TN)),
        ],
        axis=0,
    ).astype(BF)
    piece = lbuf.shape[1]
    for j in range(inner):
        lbuf[j] = l_rows[j * piece : (j + 1) * piece]
    l_copies = scatter(lbuf, lrecv, l_sem)
    pair_row = jnp.sum(jnp.where(diagonal, pair_terms[0], 0.0), axis=0, keepdims=True)
    pair_own = jnp.sum(jnp.where(picker, pair_row, 0.0), axis=1, keepdims=True)
    pair_own = jnp.broadcast_to(pair_own, (channels, lanes))
    precv[0] = pair_own.astype(BF)
    p_copies = [send(precv.at[0], precv.at[k], lp_sem, (k - 1,), inner_peer(k)) for k in range(1, inner)]

    total = exchange_outer(total_of(e_copies, ebuf[own].astype(F32), erecv), 0)
    eg_copies = gather(eres, total, eg_sem)
    total = exchange_outer(total_of(l_copies, lbuf[own].astype(F32), lrecv), 1)
    lg_copies = gather(lres, total, lg_sem)
    for k in range(1, inner):
        p_copies[k - 1].wait_recv()
        pair_own = pair_own + precv[k].astype(F32)
    pair_own = exchange_outer(pair_own, 2)
    gpair_out[...] = pair_own[:, 0:1] * factor

    def arrived(copies, res):
        for k in range(1, inner):
            copies[k - 1].wait_recv()
        return jnp.concatenate([res[j] for j in range(inner)], axis=0).astype(F32) * factor

    whole = arrived(eg_copies, eres)
    gtok_out[...] = whole[0:token_cols].T
    gout_out[...] = whole[token_cols : token_cols + depth]
    whole = arrived(lg_copies, lres)
    for f in range(4):
        gproj_out[f] = whole[f * depth : (f + 1) * depth].T
    for copy in sends:
        copy.wait_send()


def on_device(atom_feats, pair_feats, tok_slot, w_proj, w_out, w_pair, w_tok, d_tok):
    samples, atoms, width = atom_feats.shape
    depth = w_proj.shape[2]
    lanes = width
    groups = lanes // depth
    step = groups * Q_WIN
    chunks = atoms // step
    rows = samples * Q_WIN
    blocks = chunks * groups
    slots, token_cols = d_tok.shape[1], d_tok.shape[2]
    channels = w_pair.shape[0]
    n = lax.axis_size("slab")
    heads = lax.axis_size("head")
    inner = next(m for m in (8, 4, 2, 1) if n % m == 0)
    outer = n // inner
    e_piece = -(-(token_cols + depth) // (16 * inner)) * 16
    l_piece = -(-(4 * depth) // (16 * inner)) * 16
    peers = max(inner - 1, 1)
    far = max(outer - 1, 1)

    def vm(*shape, dtype=BF):
        return pltpu.VMEM(shape, dtype)

    def sems(*shape):
        return pltpu.SemaphoreType.DMA((2,) + shape)

    packed = chunks * rows
    scratch = [
        vm(atoms * channels, K_WIN),
        vm(2, samples, RIM, width),
        vm(samples, atoms + 2 * RIM, width),
        vm(heads, depth, width),
        vm(heads * lanes, groups * lanes),
        vm(groups * lanes, 2 * lanes),
        vm(groups * lanes, lanes),
        vm(groups * lanes, lanes),
        vm(blocks, Q_WIN, K_WIN, dtype=F32),
        vm(packed, groups * lanes),
        vm(packed, lanes, dtype=F32),
        vm(packed, lanes),
        vm(packed, groups * lanes),
        vm(samples, blocks, Q_WIN, K_WIN, dtype=F32),
        vm(packed, groups * lanes),
        vm(packed, lanes, dtype=F32),
        vm(heads, chunks, rows, lanes),
        vm(samples, atoms, width),
        vm(samples, atoms, token_cols),
        vm(samples, atoms, token_cols),
        vm(packed, groups * lanes),
        vm(chunks, rows, lanes, dtype=F32),
        vm(heads - 1, chunks, rows, lanes),
        vm(heads - 1, chunks, rows, lanes),
        vm(packed, lanes),
        vm(packed, lanes),
        vm(packed, lanes),
        vm(packed, groups * lanes),
        vm(heads - 1, depth, lanes),
        vm(heads - 1, depth, lanes),
        vm(inner, e_piece, lanes),
        vm(peers, e_piece, lanes),
        vm(inner, e_piece, lanes),
        vm(inner, l_piece, lanes),
        vm(peers, l_piece, lanes),
        vm(inner, channels, lanes),
        vm(inner, l_piece, lanes),
        vm(3, outer, max(e_piece, l_piece, channels), lanes),
        pltpu.SemaphoreType.DMA,
        sems(2),
        sems(heads - 1),
        sems(heads - 1, chunks),
        sems(heads - 1, chunks),
        sems(heads - 1),
        sems(peers),
        sems(peers),
        sems(peers),
        sems(peers),
        sems(peers),
        sems(3, far),
    ]
    in_vmem = pl.BlockSpec(memory_space=pltpu.VMEM)
    return pl.pallas_call(
        functools.partial(kernel, n, heads, inner),
        out_shape=(
            jax.ShapeDtypeStruct((samples, slots, token_cols), BF),
            jax.ShapeDtypeStruct((4, width, depth), F32),
            jax.ShapeDtypeStruct((depth, width), F32),
            jax.ShapeDtypeStruct((channels, 1), F32),
            jax.ShapeDtypeStruct((width, token_cols), F32),
        ),
        in_specs=[in_vmem, pl.BlockSpec(memory_space=pl.ANY)] + [in_vmem] * 6,
        out_specs=[in_vmem] * 5,
        scratch_shapes=scratch,
        compiler_params=pltpu.CompilerParams(
            collective_id=0, has_side_effects=True, vmem_limit_bytes=48 * 1024 * 1024
        ),
    )(
        atom_feats,
        pair_feats.reshape(atoms * channels, K_WIN),
        tok_slot.reshape(1, atoms),
        w_proj,
        w_out,
        w_pair,
        w_tok,
        d_tok,
    )


def solution(mesh):
    return jax.shard_map(
        on_device,
        mesh=mesh,
        in_specs=(
            P(None, "slab", None),
            P("slab", None, None),
            P("slab"),
            P(None, None, "head"),
            P("head", None),
            P(None, "head"),
            P(None, "head"),
            P(None, "slab", "head"),
        ),
        out_specs=(
            P(None, "slab", "head"),
            P(None, None, "head"),
            P("head", None),
            P(None, "head"),
            P(None, "head"),
        ),
        check_vma=False,
    )
```

```python
import functools
import jax
import jax.numpy as jnp
from jax import lax
from jax.experimental import pallas as pl
from jax.experimental.pallas import tpu as pltpu
from jax.sharding import PartitionSpec as P

Q_WIN = 32
K_WIN = 128
RIM = 48
EPSILON = 1e-05
MASKED = -1e30
BF = jnp.bfloat16
F32 = jnp.float32
NT = (((1,), (1,)), ((), ()))
NN = (((1,), (0,)), ((), ()))
TN = (((0,), (0,)), ((), ()))


def mm(a, b, dims=NN):
    return lax.dot_general(a, b, dims, preferred_element_type=F32)


def iota(shape, dim):
    return lax.broadcasted_iota(jnp.int32, shape, dim)


def layer_norm(x):
    x = x.astype(F32)
    centered = x - jnp.mean(x, axis=-1, keepdims=True)
    variance = jnp.mean(centered * centered, axis=-1, keepdims=True)
    return (centered * lax.rsqrt(variance + EPSILON)).astype(BF)


def kernel(
    n, heads, inner,
    feats_in, pair_in, slot_in, wproj_in, wout_in, wpair_in, wtok_in, dtok_in,
    tok_out, gproj_out, gout_out, gpair_out, gtok_out,
    feats, pair, slot, wproj, wout, wpair, wtok, dtok, halo, nx, wo, wbig, bdqg, bdk, bdv, bias, ncat, gate, qp, ucat, prob, zcat, att,
    hbuf, mhs, acts, ags, mtc, og0, osend, orecv, agp, ggp, qgp, ycat,
    gosend, gorecv, ebuf, erecv, eres, lbuf, lrecv, precv, lres, xbuf,
    in_sem, halo_sem, wo_sem, h_sem, o_sem, go_sem, e_sem, eg_sem, l_sem, lp_sem, lg_sem, x_sem,
):
    samples, atoms, width = feats.shape
    depth = wproj.shape[1]
    lanes = width
    groups = lanes // depth
    step = groups * Q_WIN
    chunks = atoms // step
    rows = samples * Q_WIN
    slots = dtok.shape[1]
    channels = wpair.shape[1]
    token_cols = wtok.shape[0]
    scale = depth ** (-0.5)
    factor = (samples * atoms * n) ** (-0.5)
    outer = n // inner
    me_s = lax.axis_index("slab")
    me_h = lax.axis_index("head")
    own = lax.rem(me_s, inner)
    base = me_s - own
    sends = []

    def head_peer(k):
        return {"head": lax.rem(me_h + k + heads, heads)}

    def inner_peer(k):
        return {"slab": base + lax.rem(own + k, inner)}

    def outer_peer(k):
        return {"slab": lax.rem(me_s + k * inner, n)}

    def ring_peer(k):
        return {"slab": lax.rem(me_s + k + n, n)}

    def send(src, dst, sems, index, device):
        copy = pltpu.make_async_remote_copy(
            src_ref=src, dst_ref=dst, send_sem=sems.at[(0,) + index], recv_sem=sems.at[(1,) + index],
            device_id=device, device_id_type=pl.DeviceIdType.MESH,
        )
        copy.start()
        sends.append(copy)
        return copy

    ins = (feats_in, wproj_in, wout_in, slot_in, dtok_in, wpair_in, wtok_in, pair_in)
    kept = (feats, wproj, wout, slot, dtok, wpair, wtok, pair)
    loads = [pltpu.make_async_copy(a, b, in_sem.at[i]) for i, (a, b) in enumerate(zip(ins, kept))]
    for load in loads:
        load.start()
    greeted = [head_peer(k) for k in range(1, heads)] + [inner_peer(k) for k in range(1, inner)]
    greeted += [outer_peer(k) for k in range(1, outer)]
    if outer > 1:
        greeted += [ring_peer(1), ring_peer(-1)]
    barrier = pltpu.get_barrier_semaphore()
    for device in greeted:
        pl.semaphore_signal(barrier, inc=1, device_id=device, device_id_type=pl.DeviceIdType.MESH)

    loads[0].wait()
    for s in range(samples):
        nx[s, RIM : RIM + atoms, :] = layer_norm(feats[s])
    loads[1].wait()
    loads[2].wait()
    lane_group = iota((lanes, lanes), 1) // depth
    row_group = iota((lanes, lanes), 0) // depth
    spreader = (lax.rem(iota((depth, lanes), 1), depth) == iota((depth, lanes), 0)).astype(F32).astype(BF)
    wide = [mm(wproj[f], spreader, TN) for f in range(4)]
    for g in range(groups):
        keep = lane_group == g
        span = slice(g * lanes, (g + 1) * lanes)
        bdqg[span, :lanes] = jnp.where(keep, wide[0], 0.0).astype(BF)
        bdqg[span, lanes:] = jnp.where(keep, wide[3], 0.0).astype(BF)
        bdk[span, :] = jnp.where(keep, wide[1], 0.0).astype(BF)
        bdv[span, :] = jnp.where(keep, wide[2], 0.0).astype(BF)
    wo[0] = wout[...]

    pl.semaphore_wait(barrier, len(greeted))

    to_left = send(feats.at[:, 0:RIM, :], halo.at[1], halo_sem, (1,), ring_peer(-1))
    to_right = send(feats.at[:, atoms - RIM : atoms, :], halo.at[0], halo_sem, (0,), ring_peer(1))
    wo_copies = [send(wout, wo.at[k], wo_sem, (k - 1,), head_peer(k)) for k in range(1, heads)]

    for c in range(chunks):
        for s in range(samples):
            for g in range(groups):
                at = RIM + c * step + g * Q_WIN
                ncat[c * rows + s * Q_WIN : c * rows + (s + 1) * Q_WIN, g * lanes : (g + 1) * lanes] = nx[
                    s, at : at + Q_WIN, :
                ]
    projected = mm(ncat[...], bdqg[...])
    queries = (projected[:, :lanes] * scale).astype(BF)
    qp[...] = queries
    gate[...] = jax.nn.sigmoid(projected[:, lanes:])
    ucat[...] = mm(queries, bdk[...], NT).astype(BF)

    for i in (3, 4, 5, 6):
        loads[i].wait()
    slot_ids = me_s * slots + iota((slots, atoms), 0)
    member = jnp.where(slot[...] == slot_ids, 1.0, 0.0)
    divisor = jnp.maximum(jnp.sum(member, axis=1, keepdims=True), 1.0)
    member = member.astype(BF)
    tok_grad = [(dtok[s].astype(F32) / divisor).astype(BF) for s in range(samples)]

    flat = Q_WIN * channels
    picker = lax.rem(iota((channels, flat), 1), channels) == iota((channels, flat), 0)
    w_wide = jnp.broadcast_to(wpair[...].astype(F32), (Q_WIN, channels)).astype(BF)
    w_rows = mm(w_wide, picker.astype(F32).astype(BF))
    diagonal = iota((Q_WIN, flat), 1) // channels == iota((Q_WIN, flat), 0)
    mixer = jnp.where(diagonal, w_rows, 0.0).astype(BF)
    loads[7].wait()
    for b in range(chunks * groups):
        bias[b] = mm(mixer, pair[b * flat : (b + 1) * flat, :])

    for k in range(heads):
        if k:
            wo_copies[k - 1].wait_recv()
        tall = jnp.concatenate([wo[k]] * groups, axis=0).astype(F32)
        for g in range(groups):
            wbig[k * lanes : (k + 1) * lanes, g * lanes : (g + 1) * lanes] = jnp.where(
                row_group == g, tall, 0.0
            ).astype(BF)

    to_right.wait_recv()
    to_left.wait_recv()
    for s in range(samples):
        nx[s, 0:RIM, :] = layer_norm(halo[0, s])
        nx[s, RIM + atoms : RIM + atoms + RIM, :] = layer_norm(halo[1, s])

    h_copies, o_copies = {}, {}

    def forward(c):
        at_rows = slice(c * rows, (c + 1) * rows)
        for s in range(samples):
            for g in range(groups):
                b = c * groups + g
                cols = slice(g * lanes, (g + 1) * lanes)
                here = slice(c * rows + s * Q_WIN, c * rows + (s + 1) * Q_WIN)
                window = nx[s, b * Q_WIN : b * Q_WIN + K_WIN, :]
                scores = mm(ucat[here, cols], window, NT) + bias[b]
                first = b * Q_WIN - RIM
                if first < 0 or first + K_WIN > atoms:
                    where = me_s * atoms + first + iota((Q_WIN, K_WIN), 1)
                    scores = jnp.where((where >= 0) & (where < atoms * n), scores, MASKED)
                top = jnp.max(scores, axis=1, keepdims=True)
                e = jnp.exp(scores - top)
                p = e / jnp.sum(e, axis=1, keepdims=True)
                prob[s, b] = p
                zcat[here, cols] = mm(p.astype(BF), window).astype(BF)
        attended = mm(zcat[at_rows, :], bdv[...])
        att[at_rows, :] = attended
        hbuf[0, c] = (gate[at_rows, :] * attended).astype(BF)
        h_copies[c] = [
            send(hbuf.at[0, c], hbuf.at[k, c], h_sem, (k - 1, c), head_peer(k)) for k in range(1, heads)
        ]

    def middle(c):
        for copy in h_copies[c]:
            copy.wait_recv()
        mixed = mm(jnp.concatenate([hbuf[k, c] for k in range(heads)], axis=1), wbig[...])
        for s in range(samples):
            parts = [mixed[s * Q_WIN : (s + 1) * Q_WIN, g * lanes : (g + 1) * lanes] for g in range(groups)]
            span = slice(c * step, (c + 1) * step)
            half = (feats[s, span, :].astype(F32) + jnp.concatenate(parts, axis=0)).astype(BF)
            mhs[s, span, :] = half
            pre = mm(half, wtok[...], NT)
            g1 = jax.nn.sigmoid(pre)
            acts[s, span, :] = (pre * g1).astype(BF)
            spread = mm(member[:, span], tok_grad[s], TN)
            ag = (spread * (g1 * (1.0 + pre * (1.0 - g1)))).astype(BF)
            ags[s, span, :] = ag
            mt = mm(ag, wtok[...]).astype(BF)
            for g in range(groups):
                mtc[c * rows + s * Q_WIN : c * rows + (s + 1) * Q_WIN, g * lanes : (g + 1) * lanes] = mt[
                    g * Q_WIN : (g + 1) * Q_WIN, :
                ]
        og = mm(mtc[c * rows : (c + 1) * rows, :], wbig[...], NT)
        og0[c] = og[:, :lanes]
        o_copies[c] = []
        for k in range(1, heads):
            osend[k - 1, c] = og[:, k * lanes : (k + 1) * lanes].astype(BF)
            o_copies[c].append(send(osend.at[k - 1, c], orecv.at[k - 1, c], o_sem, (k - 1, c), head_peer(-k)))

    def diagonal_sum(a):
        total = a[0:depth, 0:lanes]
        for g in range(1, groups):
            total = total + a[g * depth : (g + 1) * depth, g * lanes : (g + 1) * lanes]
        return total

    pair_terms = [None]

    def backward(c):
        at_rows = slice(c * rows, (c + 1) * rows)
        for copy in o_copies[c]:
            copy.wait_recv()
        og = og0[c]
        for k in range(1, heads):
            og = og + orecv[k - 1, c].astype(F32)
        gt = gate[at_rows, :]
        ag = (gt * og).astype(BF)
        agp[at_rows, :] = ag
        ggp[at_rows, :] = (og * att[at_rows, :] * gt * (1.0 - gt)).astype(BF)
        tcat = mm(ag, bdv[...], NT).astype(BF)
        for g in range(groups):
            b = c * groups + g
            cols = slice(g * lanes, (g + 1) * lanes)
            both = None
            for s in range(samples):
                here = slice(c * rows + s * Q_WIN, c * rows + (s + 1) * Q_WIN)
                window = nx[s, b * Q_WIN : b * Q_WIN + K_WIN, :]
                dp = mm(tcat[s * Q_WIN : (s + 1) * Q_WIN, cols], window, NT)
                p = prob[s, b]
                ds = (p * (dp - jnp.sum(p * dp, axis=1, keepdims=True))).astype(BF)
                ycat[here, cols] = mm(ds, window).astype(BF)
                ds = ds.astype(F32)
                both = ds if both is None else both + ds
            term = mm(both.astype(BF), pair[b * flat : (b + 1) * flat, :], NT)
            pair_terms[0] = term if pair_terms[0] is None else pair_terms[0] + term
        qgp[at_rows, :] = (scale * mm(ycat[at_rows, :], bdk[...])).astype(BF)

    order = []
    for t in range(chunks + 3):
        if t < chunks:
            order.append((forward, t))
        if 0 <= t - 1 < chunks:
            order.append((middle, t - 1))
        if t - 3 >= 0:
            order.append((backward, t - 3))
    late = [entry for entry in order if entry[0] is backward][1:]
    for step_of, c in [entry for entry in order if entry not in late]:
        step_of(c)

    hcat = jnp.concatenate(
        [jnp.concatenate([hbuf[k, c] for c in range(chunks)], axis=0) for k in range(heads)], axis=1
    )
    go_copies = []
    cross = mm(hcat, mtc[...], TN)
    go_own = diagonal_sum(cross[0:lanes])
    for k in range(1, heads):
        gosend[k - 1] = diagonal_sum(cross[k * lanes : (k + 1) * lanes]).astype(BF)
        go_copies.append(send(gosend.at[k - 1], gorecv.at[k - 1], go_sem, (k - 1,), head_peer(-k)))

    gtok = None
    for s in range(samples):
        sums = mm(member, acts[s])
        tok_out[s] = (sums / divisor).astype(BF)
        term = mm(ags[s], mhs[s], TN)
        gtok = term if gtok is None else gtok + term

    half_late = len(late) // 2
    for step_of, c in late[:half_late]:
        step_of(c)

    def exchange_outer(value, where):
        if outer == 1:
            return value
        xbuf[where, 0, : value.shape[0], :] = value.astype(BF)
        copies = [
            send(xbuf.at[where, 0], xbuf.at[where, k], x_sem, (where, k - 1), outer_peer(k)) for k in range(1, outer)
        ]
        for k in range(1, outer):
            copies[k - 1].wait_recv()
            value = value + xbuf[where, k, : value.shape[0], :].astype(F32)
        return value

    def scatter(buf, recv, sems):
        return [
            send(buf.at[lax.rem(own + k, inner)], recv.at[k - 1], sems, (k - 1,), inner_peer(k))
            for k in range(1, inner)
        ]

    def total_of(copies, value, recv):
        for k in range(1, inner):
            copies[k - 1].wait_recv()
            value = value + recv[k - 1].astype(F32)
        return value

    def gather(res, value, sems):
        res[own] = value.astype(BF)
        return [send(res.at[own], res.at[own], sems, (k - 1,), inner_peer(k)) for k in range(1, inner)]

    for k in range(1, heads):
        go_copies[k - 1].wait_recv()
        go_own = go_own + gorecv[k - 1].astype(F32)
    piece = ebuf.shape[1]
    parts = [gtok, go_own]
    spare = inner * piece - token_cols - depth
    if spare:
        parts.append(jnp.zeros((spare, lanes), F32))
    e_rows = jnp.concatenate(parts, axis=0).astype(BF)
    for j in range(inner):
        ebuf[j] = e_rows[j * piece : (j + 1) * piece]
    e_copies = scatter(ebuf, erecv, e_sem)

    for step_of, c in late[half_late:]:
        step_of(c)

    l_rows = jnp.concatenate(
        [
            diagonal_sum(mm(qgp[...], ncat[...], TN)),
            diagonal_sum(mm(qp[...], ycat[...], TN)),
            diagonal_sum(mm(agp[...], zcat[...], TN)),
            diagonal_sum(mm(ggp[...], ncat[...], TN)),
        ],
        axis=0,
    ).astype(BF)
    piece = lbuf.shape[1]
    for j in range(inner):
        lbuf[j] = l_rows[j * piece : (j + 1) * piece]
    l_copies = scatter(lbuf, lrecv, l_sem)
    pair_row = jnp.sum(jnp.where(diagonal, pair_terms[0], 0.0), axis=0, keepdims=True)
    pair_own = jnp.sum(jnp.where(picker, pair_row, 0.0), axis=1, keepdims=True)
    pair_own = jnp.broadcast_to(pair_own, (channels, lanes))
    precv[0] = pair_own.astype(BF)
    p_copies = [send(precv.at[0], precv.at[k], lp_sem, (k - 1,), inner_peer(k)) for k in range(1, inner)]

    total = exchange_outer(total_of(e_copies, ebuf[own].astype(F32), erecv), 0)
    eg_copies = gather(eres, total, eg_sem)
    total = exchange_outer(total_of(l_copies, lbuf[own].astype(F32), lrecv), 1)
    lg_copies = gather(lres, total, lg_sem)
    for k in range(1, inner):
        p_copies[k - 1].wait_recv()
        pair_own = pair_own + precv[k].astype(F32)
    pair_own = exchange_outer(pair_own, 2)
    across = iota((channels, lanes), 0) == iota((channels, lanes), 1)
    pair_row = jnp.sum(jnp.where(across, pair_own, 0.0), axis=0, keepdims=True)
    gpair_out[...] = pair_row[:, :channels] * factor

    def arrived(copies, res):
        for k in range(1, inner):
            copies[k - 1].wait_recv()
        return jnp.concatenate([res[j] for j in range(inner)], axis=0).astype(F32) * factor

    whole = arrived(eg_copies, eres)
    gtok_out[...] = whole[0:token_cols]
    gout_out[...] = whole[token_cols : token_cols + depth]
    whole = arrived(lg_copies, lres)
    for f in range(4):
        gproj_out[f] = whole[f * depth : (f + 1) * depth]
    for copy in sends:
        copy.wait_send()


def on_device(atom_feats, pair_feats, tok_slot, w_proj, w_out, w_pair, w_tok, d_tok):
    samples, atoms, width = atom_feats.shape
    depth = w_proj.shape[2]
    lanes = width
    groups = lanes // depth
    step = groups * Q_WIN
    chunks = atoms // step
    rows = samples * Q_WIN
    blocks = chunks * groups
    slots, token_cols = d_tok.shape[1], d_tok.shape[2]
    channels = w_pair.shape[0]
    n = lax.axis_size("slab")
    heads = lax.axis_size("head")
    inner = next(m for m in (8, 4, 2, 1) if n % m == 0)
    outer = n // inner
    e_piece = -(-(token_cols + depth) // (16 * inner)) * 16
    l_piece = -(-(4 * depth) // (16 * inner)) * 16
    peers = max(inner - 1, 1)
    far = max(outer - 1, 1)

    def vm(*shape, dtype=BF):
        return pltpu.VMEM(shape, dtype)

    def sems(*shape):
        return pltpu.SemaphoreType.DMA((2,) + shape)

    packed = chunks * rows
    scratch = [
        vm(samples, atoms, width),
        vm(atoms * channels, K_WIN),
        vm(1, atoms, dtype=jnp.int32),
        vm(4, depth, width),
        vm(depth, width),
        vm(1, channels),
        vm(token_cols, width),
        vm(samples, slots, token_cols),
        vm(2, samples, RIM, width),
        vm(samples, atoms + 2 * RIM, width),
        vm(heads, depth, width),
        vm(heads * lanes, groups * lanes),
        vm(groups * lanes, 2 * lanes),
        vm(groups * lanes, lanes),
        vm(groups * lanes, lanes),
        vm(blocks, Q_WIN, K_WIN, dtype=F32),
        vm(packed, groups * lanes),
        vm(packed, lanes, dtype=F32),
        vm(packed, lanes),
        vm(packed, groups * lanes),
        vm(samples, blocks, Q_WIN, K_WIN, dtype=F32),
        vm(packed, groups * lanes),
        vm(packed, lanes, dtype=F32),
        vm(heads, chunks, rows, lanes),
        vm(samples, atoms, width),
        vm(samples, atoms, token_cols),
        vm(samples, atoms, token_cols),
        vm(packed, groups * lanes),
        vm(chunks, rows, lanes, dtype=F32),
        vm(heads - 1, chunks, rows, lanes),
        vm(heads - 1, chunks, rows, lanes),
        vm(packed, lanes),
        vm(packed, lanes),
        vm(packed, lanes),
        vm(packed, groups * lanes),
        vm(heads - 1, depth, lanes),
        vm(heads - 1, depth, lanes),
        vm(inner, e_piece, lanes),
        vm(peers, e_piece, lanes),
        vm(inner, e_piece, lanes),
        vm(inner, l_piece, lanes),
        vm(peers, l_piece, lanes),
        vm(inner, channels, lanes),
        vm(inner, l_piece, lanes),
        vm(3, outer, max(e_piece, l_piece, channels), lanes),
        pltpu.SemaphoreType.DMA((8,)),
        sems(2),
        sems(heads - 1),
        sems(heads - 1, chunks),
        sems(heads - 1, chunks),
        sems(heads - 1),
        sems(peers),
        sems(peers),
        sems(peers),
        sems(peers),
        sems(peers),
        sems(3, far),
    ]
    in_vmem = pl.BlockSpec(memory_space=pltpu.VMEM)
    in_hbm = pl.BlockSpec(memory_space=pltpu.HBM)
    shapes = (
        jax.ShapeDtypeStruct((samples, slots, token_cols), BF),
        jax.ShapeDtypeStruct((4, depth, width), F32),
        jax.ShapeDtypeStruct((depth, width), F32),
        jax.ShapeDtypeStruct((1, channels), F32),
        jax.ShapeDtypeStruct((token_cols, width), F32),
    )
    results = pl.pallas_call(
        functools.partial(kernel, n, heads, inner),
        out_shape=shapes,
        in_specs=[in_hbm] * 8,
        out_specs=[in_vmem] * 5,
        scratch_shapes=scratch,
        compiler_params=pltpu.CompilerParams(
            collective_id=0, has_side_effects=True, vmem_limit_bytes=67043328
        ),
    )(
        atom_feats,
        pair_feats.reshape(atoms * channels, K_WIN),
        tok_slot.reshape(1, atoms),
        jnp.swapaxes(w_proj, 1, 2),
        w_out,
        w_pair.T,
        w_tok.T,
        d_tok,
    )
    tok_act, grad_proj, grad_out, grad_pair, grad_tok = pl.pallas_call(
        store,
        out_shape=shapes,
        in_specs=[in_vmem] * 5,
        out_specs=[in_hbm] * 5,
        scratch_shapes=[pltpu.SemaphoreType.DMA((5,))],
    )(*results)
    return tok_act, jnp.swapaxes(grad_proj, 1, 2), grad_out, grad_pair.T, grad_tok.T


def store(*refs):
    sem = refs[10]
    copies = [pltpu.make_async_copy(refs[i], refs[5 + i], sem.at[i]) for i in range(5)]
    for copy in copies:
        copy.start()
    for copy in copies:
        copy.wait()


def solution(mesh):
    return jax.shard_map(
        on_device,
        mesh=mesh,
        in_specs=(
            P(None, "slab", None),
            P("slab", None, None),
            P("slab"),
            P(None, None, "head"),
            P("head", None),
            P(None, "head"),
            P(None, "head"),
            P(None, "slab", "head"),
        ),
        out_specs=(
            P(None, "slab", "head"),
            P(None, None, "head"),
            P("head", None),
            P(None, "head"),
            P(None, "head"),
        ),
        check_vma=False,
    )
```

```python
import functools
import jax
import jax.numpy as jnp
from jax import lax
from jax.experimental import pallas as pl
from jax.experimental.pallas import tpu as pltpu
from jax.sharding import PartitionSpec as P

Q_WIN = 32
K_WIN = 128
RIM = 48
EPSILON = 1e-05
MASKED = -1e30
BF = jnp.bfloat16
F32 = jnp.float32
NT = (((1,), (1,)), ((), ()))
NN = (((1,), (0,)), ((), ()))
TN = (((0,), (0,)), ((), ()))


def mm(a, b, dims=NN):
    return lax.dot_general(a, b, dims, preferred_element_type=F32)


def iota(shape, dim):
    return lax.broadcasted_iota(jnp.int32, shape, dim)


def layer_norm(x):
    x = x.astype(F32)
    centered = x - jnp.mean(x, axis=-1, keepdims=True)
    variance = jnp.mean(centered * centered, axis=-1, keepdims=True)
    return (centered * lax.rsqrt(variance + EPSILON)).astype(BF)


def kernel(
    n, heads, inner,
    feats_in, pair_in, slot_in, wproj_in, wout_in, wpair_in, wtok_in, dtok_in,
    tok_out, gproj_out, gout_out, gpair_out, gtok_out,
    feats, pair, slot, wproj, wout, wpair, wtok, dtok, halo, nx, wo, wbig, bdqg, bdk, bdv, bias, ncat, gate, qp, ucat, prob, zcat, att,
    hbuf, mhs, acts, ags, mtc, og0, osend, orecv, agp, ggp, qgp, ycat,
    gosend, gorecv, ebuf, erecv, eres, lbuf, lrecv, precv, lres, xbuf,
    in_sem, halo_sem, wo_sem, h_sem, o_sem, go_sem, e_sem, eg_sem, l_sem, lp_sem, lg_sem, x_sem,
):
    samples, atoms, width = feats.shape
    depth = wproj.shape[1]
    lanes = width
    groups = lanes // depth
    step = groups * Q_WIN
    chunks = atoms // step
    rows = samples * Q_WIN
    slots = dtok.shape[1]
    channels = wpair.shape[1]
    token_cols = wtok.shape[0]
    scale = depth ** (-0.5)
    factor = (samples * atoms * n) ** (-0.5)
    outer = n // inner
    me_s = lax.axis_index("slab")
    me_h = lax.axis_index("head")
    own = lax.rem(me_s, inner)
    base = me_s - own
    sends = []

    def head_peer(k):
        return {"head": lax.rem(me_h + k + heads, heads)}

    def inner_peer(k):
        return {"slab": base + lax.rem(own + k, inner)}

    def outer_peer(k):
        return {"slab": lax.rem(me_s + k * inner, n)}

    def ring_peer(k):
        return {"slab": lax.rem(me_s + k + n, n)}

    def send(src, dst, sems, index, device):
        copy = pltpu.make_async_remote_copy(
            src_ref=src, dst_ref=dst, send_sem=sems.at[(0,) + index], recv_sem=sems.at[(1,) + index],
            device_id=device, device_id_type=pl.DeviceIdType.MESH,
        )
        copy.start()
        sends.append(copy)
        return copy

    ins = (feats_in, wproj_in, wout_in, slot_in, dtok_in, wpair_in, wtok_in, pair_in)
    kept = (feats, wproj, wout, slot, dtok, wpair, wtok, pair)
    loads = [pltpu.make_async_copy(a, b, in_sem.at[i]) for i, (a, b) in enumerate(zip(ins, kept))]
    for load in loads:
        load.start()
    greeted = [head_peer(k) for k in range(1, heads)] + [inner_peer(k) for k in range(1, inner)]
    greeted += [outer_peer(k) for k in range(1, outer)]
    if outer > 1:
        greeted += [ring_peer(1), ring_peer(-1)]
    barrier = pltpu.get_barrier_semaphore()
    for device in greeted:
        pl.semaphore_signal(barrier, inc=1, device_id=device, device_id_type=pl.DeviceIdType.MESH)

    loads[0].wait()
    for s in range(samples):
        nx[s, RIM : RIM + atoms, :] = layer_norm(feats[s])
    loads[1].wait()
    loads[2].wait()
    lane_group = iota((lanes, lanes), 1) // depth
    row_group = iota((lanes, lanes), 0) // depth
    spreader = (lax.rem(iota((depth, lanes), 1), depth) == iota((depth, lanes), 0)).astype(F32).astype(BF)
    wide = [mm(wproj[f], spreader, TN) for f in range(4)]
    for g in range(groups):
        keep = lane_group == g
        span = slice(g * lanes, (g + 1) * lanes)
        bdqg[span, :lanes] = jnp.where(keep, wide[0], 0.0).astype(BF)
        bdqg[span, lanes:] = jnp.where(keep, wide[3], 0.0).astype(BF)
        bdk[span, :] = jnp.where(keep, wide[1], 0.0).astype(BF)
        bdv[span, :] = jnp.where(keep, wide[2], 0.0).astype(BF)
    wo[0] = wout[...]

    for c in range(chunks):
        for s in range(samples):
            for g in range(groups):
                at = RIM + c * step + g * Q_WIN
                ncat[c * rows + s * Q_WIN : c * rows + (s + 1) * Q_WIN, g * lanes : (g + 1) * lanes] = nx[
                    s, at : at + Q_WIN, :
                ]
    projected = mm(ncat[...], bdqg[...])
    queries = (projected[:, :lanes] * scale).astype(BF)
    qp[...] = queries
    gate[...] = jax.nn.sigmoid(projected[:, lanes:])
    ucat[...] = mm(queries, bdk[...], NT).astype(BF)

    for i in (3, 4, 5, 6):
        loads[i].wait()
    slot_ids = me_s * slots + iota((slots, atoms), 0)
    member = jnp.where(slot[...] == slot_ids, 1.0, 0.0)
    divisor = jnp.maximum(jnp.sum(member, axis=1, keepdims=True), 1.0)
    member = member.astype(BF)
    tok_grad = [(dtok[s].astype(F32) / divisor).astype(BF) for s in range(samples)]

    flat = Q_WIN * channels
    picker = lax.rem(iota((channels, flat), 1), channels) == iota((channels, flat), 0)
    w_wide = jnp.broadcast_to(wpair[...].astype(F32), (Q_WIN, channels)).astype(BF)
    w_rows = mm(w_wide, picker.astype(F32).astype(BF))
    diagonal = iota((Q_WIN, flat), 1) // channels == iota((Q_WIN, flat), 0)
    mixer = jnp.where(diagonal, w_rows, 0.0).astype(BF)
    loads[7].wait()
    for b in range(chunks * groups):
        bias[b] = mm(mixer, pair[b * flat : (b + 1) * flat, :])

    pl.semaphore_wait(barrier, len(greeted))

    to_left = send(feats.at[:, 0:RIM, :], halo.at[1], halo_sem, (1,), ring_peer(-1))
    to_right = send(feats.at[:, atoms - RIM : atoms, :], halo.at[0], halo_sem, (0,), ring_peer(1))
    wo_copies = [send(wout, wo.at[k], wo_sem, (k - 1,), head_peer(k)) for k in range(1, heads)]

    def output_weights():
        for k in range(heads):
            if k:
                wo_copies[k - 1].wait_recv()
            tall = jnp.concatenate([wo[k]] * groups, axis=0).astype(F32)
            for g in range(groups):
                wbig[k * lanes : (k + 1) * lanes, g * lanes : (g + 1) * lanes] = jnp.where(
                    row_group == g, tall, 0.0
                ).astype(BF)

    def halo_rows():
        to_right.wait_recv()
        to_left.wait_recv()
        for s in range(samples):
            nx[s, 0:RIM, :] = layer_norm(halo[0, s])
            nx[s, RIM + atoms : RIM + atoms + RIM, :] = layer_norm(halo[1, s])

    h_copies, o_copies = {}, {}

    def forward(c):
        at_rows = slice(c * rows, (c + 1) * rows)
        for s in range(samples):
            for g in range(groups):
                b = c * groups + g
                cols = slice(g * lanes, (g + 1) * lanes)
                here = slice(c * rows + s * Q_WIN, c * rows + (s + 1) * Q_WIN)
                window = nx[s, b * Q_WIN : b * Q_WIN + K_WIN, :]
                scores = mm(ucat[here, cols], window, NT) + bias[b]
                first = b * Q_WIN - RIM
                if first < 0 or first + K_WIN > atoms:
                    where = me_s * atoms + first + iota((Q_WIN, K_WIN), 1)
                    scores = jnp.where((where >= 0) & (where < atoms * n), scores, MASKED)
                top = jnp.max(scores, axis=1, keepdims=True)
                e = jnp.exp(scores - top)
                p = e / jnp.sum(e, axis=1, keepdims=True)
                prob[s, b] = p
                zcat[here, cols] = mm(p.astype(BF), window).astype(BF)
        attended = mm(zcat[at_rows, :], bdv[...])
        att[at_rows, :] = attended
        hbuf[0, c] = (gate[at_rows, :] * attended).astype(BF)
        h_copies[c] = [
            send(hbuf.at[0, c], hbuf.at[k, c], h_sem, (k - 1, c), head_peer(k)) for k in range(1, heads)
        ]

    def middle(c):
        for copy in h_copies[c]:
            copy.wait_recv()
        mixed = mm(jnp.concatenate([hbuf[k, c] for k in range(heads)], axis=1), wbig[...])
        for s in range(samples):
            parts = [mixed[s * Q_WIN : (s + 1) * Q_WIN, g * lanes : (g + 1) * lanes] for g in range(groups)]
            span = slice(c * step, (c + 1) * step)
            half = (feats[s, span, :].astype(F32) + jnp.concatenate(parts, axis=0)).astype(BF)
            mhs[s, span, :] = half
            pre = mm(half, wtok[...], NT)
            g1 = jax.nn.sigmoid(pre)
            acts[s, span, :] = (pre * g1).astype(BF)
            spread = mm(member[:, span], tok_grad[s], TN)
            ag = (spread * (g1 * (1.0 + pre * (1.0 - g1)))).astype(BF)
            ags[s, span, :] = ag
            mt = mm(ag, wtok[...]).astype(BF)
            for g in range(groups):
                mtc[c * rows + s * Q_WIN : c * rows + (s + 1) * Q_WIN, g * lanes : (g + 1) * lanes] = mt[
                    g * Q_WIN : (g + 1) * Q_WIN, :
                ]
        og = mm(mtc[c * rows : (c + 1) * rows, :], wbig[...], NT)
        og0[c] = og[:, :lanes]
        o_copies[c] = []
        for k in range(1, heads):
            osend[k - 1, c] = og[:, k * lanes : (k + 1) * lanes].astype(BF)
            o_copies[c].append(send(osend.at[k - 1, c], orecv.at[k - 1, c], o_sem, (k - 1, c), head_peer(-k)))

    def diagonal_sum(a):
        total = a[0:depth, 0:lanes]
        for g in range(1, groups):
            total = total + a[g * depth : (g + 1) * depth, g * lanes : (g + 1) * lanes]
        return total

    pair_terms = [None]

    def backward(c):
        at_rows = slice(c * rows, (c + 1) * rows)
        for copy in o_copies[c]:
            copy.wait_recv()
        og = og0[c]
        for k in range(1, heads):
            og = og + orecv[k - 1, c].astype(F32)
        gt = gate[at_rows, :]
        ag = (gt * og).astype(BF)
        agp[at_rows, :] = ag
        ggp[at_rows, :] = (og * att[at_rows, :] * gt * (1.0 - gt)).astype(BF)
        tcat = mm(ag, bdv[...], NT).astype(BF)
        for g in range(groups):
            b = c * groups + g
            cols = slice(g * lanes, (g + 1) * lanes)
            both = None
            for s in range(samples):
                here = slice(c * rows + s * Q_WIN, c * rows + (s + 1) * Q_WIN)
                window = nx[s, b * Q_WIN : b * Q_WIN + K_WIN, :]
                dp = mm(tcat[s * Q_WIN : (s + 1) * Q_WIN, cols], window, NT)
                p = prob[s, b]
                ds = (p * (dp - jnp.sum(p * dp, axis=1, keepdims=True))).astype(BF)
                ycat[here, cols] = mm(ds, window).astype(BF)
                ds = ds.astype(F32)
                both = ds if both is None else both + ds
            term = mm(both.astype(BF), pair[b * flat : (b + 1) * flat, :], NT)
            pair_terms[0] = term if pair_terms[0] is None else pair_terms[0] + term
        qgp[at_rows, :] = (scale * mm(ycat[at_rows, :], bdk[...])).astype(BF)

    reach = K_WIN - Q_WIN - RIM
    edges = [c for c in range(chunks) if c * step < RIM or (c + 1) * step + reach > atoms]
    turn = [c for c in range(chunks) if c not in edges] + edges
    order = []
    for t in range(chunks + 3):
        if t < chunks:
            if turn[t] == edges[0]:
                order.append((lambda c: halo_rows(), 0))
            order.append((forward, turn[t]))
        if 0 <= t - 1 < chunks:
            if t == 1:
                order.append((lambda c: output_weights(), 0))
            order.append((middle, turn[t - 1]))
        if t - 3 >= 0:
            order.append((backward, turn[t - 3]))
    late = [entry for entry in order if entry[0] is backward][1:]
    for step_of, c in [entry for entry in order if entry not in late]:
        step_of(c)

    hcat = jnp.concatenate(
        [jnp.concatenate([hbuf[k, c] for c in range(chunks)], axis=0) for k in range(heads)], axis=1
    )
    go_copies = []
    cross = mm(hcat, mtc[...], TN)
    go_own = diagonal_sum(cross[0:lanes])
    for k in range(1, heads):
        gosend[k - 1] = diagonal_sum(cross[k * lanes : (k + 1) * lanes]).astype(BF)
        go_copies.append(send(gosend.at[k - 1], gorecv.at[k - 1], go_sem, (k - 1,), head_peer(-k)))

    gtok = None
    for s in range(samples):
        sums = mm(member, acts[s])
        tok_out[s] = (sums / divisor).astype(BF)
        term = mm(ags[s], mhs[s], TN)
        gtok = term if gtok is None else gtok + term

    half_late = len(late) // 2
    for step_of, c in late[:half_late]:
        step_of(c)

    def exchange_outer(value, where):
        if outer == 1:
            return value
        xbuf[where, 0, : value.shape[0], :] = value.astype(BF)
        copies = [
            send(xbuf.at[where, 0], xbuf.at[where, k], x_sem, (where, k - 1), outer_peer(k)) for k in range(1, outer)
        ]
        for k in range(1, outer):
            copies[k - 1].wait_recv()
            value = value + xbuf[where, k, : value.shape[0], :].astype(F32)
        return value

    def scatter(buf, recv, sems):
        return [
            send(buf.at[lax.rem(own + k, inner)], recv.at[k - 1], sems, (k - 1,), inner_peer(k))
            for k in range(1, inner)
        ]

    def total_of(copies, value, recv):
        for k in range(1, inner):
            copies[k - 1].wait_recv()
            value = value + recv[k - 1].astype(F32)
        return value

    def gather(res, value, sems):
        res[own] = value.astype(BF)
        return [send(res.at[own], res.at[own], sems, (k - 1,), inner_peer(k)) for k in range(1, inner)]

    for k in range(1, heads):
        go_copies[k - 1].wait_recv()
        go_own = go_own + gorecv[k - 1].astype(F32)
    piece = ebuf.shape[1]
    parts = [gtok, go_own]
    spare = inner * piece - token_cols - depth
    if spare:
        parts.append(jnp.zeros((spare, lanes), F32))
    e_rows = jnp.concatenate(parts, axis=0).astype(BF)
    for j in range(inner):
        ebuf[j] = e_rows[j * piece : (j + 1) * piece]
    e_copies = scatter(ebuf, erecv, e_sem)

    for step_of, c in late[half_late:]:
        step_of(c)

    l_rows = jnp.concatenate(
        [
            diagonal_sum(mm(qgp[...], ncat[...], TN)),
            diagonal_sum(mm(qp[...], ycat[...], TN)),
            diagonal_sum(mm(agp[...], zcat[...], TN)),
            diagonal_sum(mm(ggp[...], ncat[...], TN)),
        ],
        axis=0,
    ).astype(BF)
    piece = lbuf.shape[1]
    for j in range(inner):
        lbuf[j] = l_rows[j * piece : (j + 1) * piece]
    l_copies = scatter(lbuf, lrecv, l_sem)
    pair_row = jnp.sum(jnp.where(diagonal, pair_terms[0], 0.0), axis=0, keepdims=True)
    pair_own = jnp.sum(jnp.where(picker, pair_row, 0.0), axis=1, keepdims=True)
    pair_own = jnp.broadcast_to(pair_own, (channels, lanes))
    precv[0] = pair_own.astype(BF)
    p_copies = [send(precv.at[0], precv.at[k], lp_sem, (k - 1,), inner_peer(k)) for k in range(1, inner)]

    total = exchange_outer(total_of(e_copies, ebuf[own].astype(F32), erecv), 0)
    eg_copies = gather(eres, total, eg_sem)
    total = exchange_outer(total_of(l_copies, lbuf[own].astype(F32), lrecv), 1)
    lg_copies = gather(lres, total, lg_sem)
    for k in range(1, inner):
        p_copies[k - 1].wait_recv()
        pair_own = pair_own + precv[k].astype(F32)
    pair_own = exchange_outer(pair_own, 2)
    across = iota((channels, lanes), 0) == iota((channels, lanes), 1)
    pair_row = jnp.sum(jnp.where(across, pair_own, 0.0), axis=0, keepdims=True)
    gpair_out[...] = pair_row[:, :channels] * factor

    def arrived(copies, res):
        for k in range(1, inner):
            copies[k - 1].wait_recv()
        return jnp.concatenate([res[j] for j in range(inner)], axis=0).astype(F32) * factor

    whole = arrived(eg_copies, eres)
    gtok_out[...] = whole[0:token_cols]
    gout_out[...] = whole[token_cols : token_cols + depth]
    whole = arrived(lg_copies, lres)
    for f in range(4):
        gproj_out[f] = whole[f * depth : (f + 1) * depth]
    for copy in sends:
        copy.wait_send()


def on_device(atom_feats, pair_feats, tok_slot, w_proj, w_out, w_pair, w_tok, d_tok):
    samples, atoms, width = atom_feats.shape
    depth = w_proj.shape[2]
    lanes = width
    groups = lanes // depth
    step = groups * Q_WIN
    chunks = atoms // step
    rows = samples * Q_WIN
    blocks = chunks * groups
    slots, token_cols = d_tok.shape[1], d_tok.shape[2]
    channels = w_pair.shape[0]
    n = lax.axis_size("slab")
    heads = lax.axis_size("head")
    inner = next(m for m in (8, 4, 2, 1) if n % m == 0)
    outer = n // inner
    e_piece = -(-(token_cols + depth) // (16 * inner)) * 16
    l_piece = -(-(4 * depth) // (16 * inner)) * 16
    peers = max(inner - 1, 1)
    far = max(outer - 1, 1)

    def vm(*shape, dtype=BF):
        return pltpu.VMEM(shape, dtype)

    def sems(*shape):
        return pltpu.SemaphoreType.DMA((2,) + shape)

    packed = chunks * rows
    scratch = [
        vm(samples, atoms, width),
        vm(atoms * channels, K_WIN),
        vm(1, atoms, dtype=jnp.int32),
        vm(4, depth, width),
        vm(depth, width),
        vm(1, channels),
        vm(token_cols, width),
        vm(samples, slots, token_cols),
        vm(2, samples, RIM, width),
        vm(samples, atoms + 2 * RIM, width),
        vm(heads, depth, width),
        vm(heads * lanes, groups * lanes),
        vm(groups * lanes, 2 * lanes),
        vm(groups * lanes, lanes),
        vm(groups * lanes, lanes),
        vm(blocks, Q_WIN, K_WIN, dtype=F32),
        vm(packed, groups * lanes),
        vm(packed, lanes, dtype=F32),
        vm(packed, lanes),
        vm(packed, groups * lanes),
        vm(samples, blocks, Q_WIN, K_WIN, dtype=F32),
        vm(packed, groups * lanes),
        vm(packed, lanes, dtype=F32),
        vm(heads, chunks, rows, lanes),
        vm(samples, atoms, width),
        vm(samples, atoms, token_cols),
        vm(samples, atoms, token_cols),
        vm(packed, groups * lanes),
        vm(chunks, rows, lanes, dtype=F32),
        vm(heads - 1, chunks, rows, lanes),
        vm(heads - 1, chunks, rows, lanes),
        vm(packed, lanes),
        vm(packed, lanes),
        vm(packed, lanes),
        vm(packed, groups * lanes),
        vm(heads - 1, depth, lanes),
        vm(heads - 1, depth, lanes),
        vm(inner, e_piece, lanes),
        vm(peers, e_piece, lanes),
        vm(inner, e_piece, lanes),
        vm(inner, l_piece, lanes),
        vm(peers, l_piece, lanes),
        vm(inner, channels, lanes),
        vm(inner, l_piece, lanes),
        vm(3, outer, max(e_piece, l_piece, channels), lanes),
        pltpu.SemaphoreType.DMA((8,)),
        sems(2),
        sems(heads - 1),
        sems(heads - 1, chunks),
        sems(heads - 1, chunks),
        sems(heads - 1),
        sems(peers),
        sems(peers),
        sems(peers),
        sems(peers),
        sems(peers),
        sems(3, far),
    ]
    in_vmem = pl.BlockSpec(memory_space=pltpu.VMEM)
    in_hbm = pl.BlockSpec(memory_space=pltpu.HBM)
    shapes = (
        jax.ShapeDtypeStruct((samples, slots, token_cols), BF),
        jax.ShapeDtypeStruct((4, depth, width), F32),
        jax.ShapeDtypeStruct((depth, width), F32),
        jax.ShapeDtypeStruct((1, channels), F32),
        jax.ShapeDtypeStruct((token_cols, width), F32),
    )
    results = pl.pallas_call(
        functools.partial(kernel, n, heads, inner),
        out_shape=shapes,
        in_specs=[in_hbm] * 8,
        out_specs=[in_vmem] * 5,
        scratch_shapes=scratch,
        compiler_params=pltpu.CompilerParams(
            collective_id=0, has_side_effects=True, vmem_limit_bytes=67043328
        ),
    )(
        atom_feats,
        pair_feats.reshape(atoms * channels, K_WIN),
        tok_slot.reshape(1, atoms),
        jnp.swapaxes(w_proj, 1, 2),
        w_out,
        w_pair.T,
        w_tok.T,
        d_tok,
    )
    tok_act, grad_proj, grad_out, grad_pair, grad_tok = pl.pallas_call(
        store,
        out_shape=shapes,
        in_specs=[in_vmem] * 5,
        out_specs=[in_hbm] * 5,
        scratch_shapes=[pltpu.SemaphoreType.DMA((5,))],
    )(*results)
    return tok_act, jnp.swapaxes(grad_proj, 1, 2), grad_out, grad_pair.T, grad_tok.T


def store(*refs):
    sem = refs[10]
    copies = [pltpu.make_async_copy(refs[i], refs[5 + i], sem.at[i]) for i in range(5)]
    for copy in copies:
        copy.start()
    for copy in copies:
        copy.wait()


def solution(mesh):
    return jax.shard_map(
        on_device,
        mesh=mesh,
        in_specs=(
            P(None, "slab", None),
            P("slab", None, None),
            P("slab"),
            P(None, None, "head"),
            P("head", None),
            P(None, "head"),
            P(None, "head"),
            P(None, "slab", "head"),
        ),
        out_specs=(
            P(None, "slab", "head"),
            P(None, None, "head"),
            P("head", None),
            P(None, "head"),
            P(None, "head"),
        ),
        check_vma=False,
    )
```
